256 devices in a mesh: chan: 64 (over x, y_hi, z), band: 4 (over y_lo, core).
Axes of the slice: x: 4, y: 4 (y_hi: 2, y_lo: 2; y = y_hi * 2 + y_lo), z: 8, core: 2. Of those that a mesh axis runs over, the one named last changes fastest.
Arguments:
- spectra: float32 [2, 32, 96, 8192], P(None, None, 'band', 'chan'), may hold values from -6 to 6
- taps: float32 [96, 16], replicated, may hold values from -2.5 to 2.5
Outputs:
- stacked: bfloat16 [8, 2, 8192, 8192], P('band', None, 'chan')
The draws below stay inside these ranges and needn't reach their ends.
All inputs are finite; a program needn't handle non-finite values.
Results may differ from the reference program's by a relative error of at most 0.0057.
Values may be sent and summed in bfloat16 or wider, within the bound.
No kernel may reach another device: no remote copies, remote signals or barrier semaphores. Data moves between devices by JAX's collectives and lax.ppermute only.
A program may use at most 192 MiB of HBM per device.

```python
import jax
import jax.numpy as jnp
from jax import lax

W = 32
F = 96
BANDS = 8
TAPS = 16
SMOOTH = 5
BAND_BINS = 12
CHANNELS = 8192


def block_scale(rng, shape, split, smallest, top_value):
    def one(position, shards_of):
        heights = jax.random.uniform(jax.random.fold_in(jax.random.fold_in(rng, 6), position), (shards_of,), jnp.float32, smallest / len(split), top_value / len(split))
        return jnp.repeat(jnp.exp(heights), shape[position] // shards_of).reshape((-1,) + (1,) * (len(shape) - position - 1))

    gain = one(*split[0])
    for cut in split[1:]:
        gain = gain * one(*cut)
    return gain


def normal_values(own_key, extent, spread, most, shards=(), dtype=jnp.bfloat16):
    values = jax.random.normal(own_key, extent, jnp.float32) * spread
    if len(shards) > 0:
        values = block_scale(own_key, extent, shards, -0.22, 0.18) * values
    return jnp.clip(values, min=-most, max=most).astype(dtype)


def setup_inputs(seed: int = 0) -> dict:
    seeds = jax.random.split(jax.random.key(seed), 3)
    spectra = normal_values(seeds[0], (2, W, F, CHANNELS), 1.0, 6.0, ((2, 4), (3, 64)), jnp.float32)
    taps = normal_values(seeds[1], (F, TAPS), 0.25, 2.5, (), jnp.float32)
    return {"spectra": spectra, "taps": taps}


water_level = 0.1

def fan_filter(extended, coeffs, width):
    result = jnp.zeros(extended.shape[:-1] + (width,), jnp.float32)
    for tap_index in range(coeffs.shape[1]):
        result = result + coeffs[:, tap_index][:, None] * extended[..., tap_index:tap_index + width]
    return result

def whiten(filtered, amp_ext, local_bins):
    smoothed = jnp.zeros(filtered.shape[1:], jnp.float32)
    for offset in range(SMOOTH):
        smoothed = smoothed + amp_ext[:, offset:offset + local_bins, :]
    smoothed = smoothed / SMOOTH
    return (filtered / (smoothed + water_level)[None]).astype(jnp.bfloat16)

def arrange(whitened, band_count):
    shaped = whitened.reshape(2, whitened.shape[1], band_count, BAND_BINS, whitened.shape[3])
    shaped = shaped.transpose(2, 0, 1, 3, 4)
    return shaped.reshape(band_count, 2 * whitened.shape[1] * BAND_BINS, whitened.shape[3])

def partner(whitened):
    return jnp.concatenate([-whitened[1:2], whitened[0:1]], axis=0)

def reference(spectra, taps):
    half_taps = TAPS // 2
    extended = jnp.concatenate([spectra[..., CHANNELS - half_taps:], spectra, spectra[..., :half_taps]], axis=3)
    filtered = fan_filter(extended, taps, CHANNELS)
    amplitude = jnp.sqrt(filtered[0] * filtered[0] + filtered[1] * filtered[1])
    reach = SMOOTH // 2
    padded = jnp.pad(amplitude, ((0, 0), (reach, reach), (0, 0)))
    whitened = whiten(filtered, padded, F)
    features = arrange(whitened, BANDS)
    rotated = arrange(partner(whitened), BANDS)
    scale_factor = 1.0 / (W * BAND_BINS)
    dims = (((0,), (0,)), ((), ()))

    def one_band(index):
        left = features[index]
        real_part = lax.dot_general(left, left, dims, preferred_element_type=jnp.float32)
        imag_part = lax.dot_general(left, rotated[index], dims, preferred_element_type=jnp.float32)
        return (jnp.stack([real_part, imag_part]) * scale_factor).astype(jnp.bfloat16)
    return lax.map(one_band, jnp.arange(BANDS))
```

```python
import functools

import jax
import jax.numpy as jnp
from jax import lax
from jax.experimental import pallas as pl
from jax.experimental.pallas import tpu as pltpu
from jax.sharding import Mesh, PartitionSpec as P


TAPS = 16
SMOOTH = 5
BAND_BINS = 12
AXES = ("x", "yh", "z", "yl", "core")
SIZES = (4, 2, 8, 2, 2)
CHAN = ("x", "yh", "z")
BAND = ("yl", "core")
BLK = 128
water_level = 0.1


def shifted(dx=0, dy=0, dz=0):
    pairs = []
    for i in range(256):
        core, yl, z, yh, x = i % 2, i // 2 % 2, i // 4 % 8, i // 32 % 2, i // 64
        y = (yh * 2 + yl + dy) % 4
        x, z = (x + dx) % 4, (z + dz) % 8
        pairs.append((i, (((x * 2 + y // 2) * 8 + z) * 2 + y % 2) * 2 + core))
    return pairs


def move(value, **delta):
    return lax.ppermute(value, AXES, shifted(**delta))


def neighbours(axes, wrap):
    devices = lax.axis_size(axes)
    up = [(i, (i + 1) % devices) for i in range(devices if wrap else devices - 1)]
    return up, [(j, i) for i, j in up]


def filter_body(x_ref, before_ref, after_ref, taps_ref, filt_ref, amp_ref):
    bins, taps = x_ref.shape[1], TAPS
    start = (lax.axis_index("yl") * 2 + lax.axis_index("core")) * bins
    lanes = lax.broadcasted_iota(jnp.int32, x_ref.shape[2:], 1)

    def one_bin(f, carry):
        power = None
        for k in range(2):
            x = x_ref[k, f]
            gap = jnp.zeros((x.shape[0], BLK - taps), jnp.float32)
            halo = jnp.concatenate([after_ref[k, f], gap, before_ref[k, f]], axis=1)
            total = jnp.zeros_like(x)
            for t in range(taps):
                lag = t - taps // 2
                if lag == 0:
                    shifted_x = x
                else:
                    inside = lanes >= lag if lag > 0 else lanes < BLK + lag
                    shifted_x = pltpu.roll(jnp.where(inside, x, halo), -lag % BLK, 1)
                total = total + taps_ref[(start + f) * taps + t] * shifted_x
            filt_ref[k, f] = total
            power = total * total if power is None else power + total * total
        amp_ref[f] = jnp.sqrt(power)
        return carry

    lax.fori_loop(0, bins, one_bin, 0)


def whiten_body(filt_ref, amp_ref, below_ref, above_ref, feat_ref, ext):
    bins, reach = amp_ref.shape[0], SMOOTH // 2
    ext[:reach] = below_ref[...]
    ext[reach : reach + bins] = amp_ref[...]
    ext[reach + bins :] = above_ref[...]
    windows = amp_ref.shape[1]

    for band in range(2):

        def one_bin(f, carry):
            g = band * BAND_BINS + f
            smoothed = jnp.zeros(amp_ref.shape[1:], jnp.float32)
            for d in range(SMOOTH):
                smoothed = smoothed + ext[g + d]
            under = smoothed / SMOOTH + water_level
            for k in range(2):
                row = pl.multiple_of((k * BAND_BINS + f) * windows, windows)
                feat_ref[band, pl.ds(row, windows)] = (filt_ref[k, g] / under).astype(jnp.bfloat16)
            return carry

        lax.fori_loop(0, BAND_BINS, one_bin, 0)


def left_body(feat_ref, left_ref):
    half = feat_ref.shape[1] // 2
    for band in range(2):
        flipped = feat_ref[band].T
        left_ref[band, :BLK] = flipped
        left_ref[band, BLK:] = jnp.concatenate([flipped[:, half:], -flipped[:, :half]], axis=1)


def simple_call(kernel, outs, ins, scratch=(), smem=()):
    vmem = pl.BlockSpec(memory_space=pltpu.VMEM)
    size = sum(v.size * v.dtype.itemsize for v in (*ins, *outs))
    return pl.pallas_call(
        kernel,
        out_shape=outs,
        in_specs=[
            pl.BlockSpec(memory_space=pltpu.SMEM) if i in smem else vmem for i in range(len(ins))
        ],
        out_specs=[vmem] * len(outs),
        scratch_shapes=list(scratch),
        cost_estimate=pl.CostEstimate(flops=4 * size, bytes_accessed=size, transcendentals=0),
        compiler_params=pltpu.CompilerParams(vmem_limit_bytes=20 << 20),
    )(*ins)


def left_rows(features):
    bands, k, c = features.shape
    return simple_call(
        left_body, [jax.ShapeDtypeStruct((bands, 2 * c, k), features.dtype)], [features]
    )[0]


def features_of(spectra, taps):
    edge, reach = TAPS // 2, SMOOTH // 2
    turned = spectra.transpose(0, 2, 1, 3)
    bins, windows, chan = turned.shape[1:]
    up, down = neighbours(CHAN, True)
    last = spectra[..., chan - edge :].transpose(0, 2, 3, 1)
    first = spectra[..., :edge].transpose(0, 2, 3, 1)
    before = lax.ppermute(last, CHAN, up).swapaxes(2, 3)
    after = lax.ppermute(first, CHAN, down).swapaxes(2, 3)
    f32 = jnp.float32
    filtered, amplitude = simple_call(
        filter_body,
        [
            jax.ShapeDtypeStruct(turned.shape, f32),
            jax.ShapeDtypeStruct((bins, windows, chan), f32),
        ],
        [turned, before, after, taps.reshape(-1)],
        smem=(3,),
    )
    up, down = neighbours(BAND, False)
    below = lax.ppermute(amplitude[bins - reach :], BAND, up)
    above = lax.ppermute(amplitude[:reach], BAND, down)
    rows = 2 * windows * BAND_BINS
    return simple_call(
        whiten_body,
        [jax.ShapeDtypeStruct((bins // BAND_BINS, rows, chan), jnp.bfloat16)],
        [filtered, amplitude, below, above],
        scratch=[pltpu.VMEM((bins + 2 * reach, windows, chan), f32)],
    )[0]


def column(dx, dz, other):
    x = lax.rem(lax.axis_index("x") + (dx % 4), 4)
    yh = lax.axis_index("yh")
    yh = 1 - yh if other else yh
    z = lax.rem(lax.axis_index("z") + (dz % 8), 8)
    return pl.multiple_of(((x * 2 + yh) * 8 + z) * BLK, BLK)


def cross_body(items, scale, n_groups, first, *refs):
    own_left, pair_left = refs[:2]
    groups = refs[2 : 2 + n_groups]
    rest = refs[2 + n_groups :] if first else refs[3 + n_groups :]
    out, sent, own, sems = rest
    copies = []
    at = 0
    for k, pair in pairs_of(items):
        band, both = pair[0][2], any(item[6] for item in pair)
        right = jnp.concatenate([groups[item[0]][item[1]] for item in pair], axis=1)
        width = len(pair) * BLK
        for side in range(2 if both else 1):
            rows = (own_left, pair_left)[side][band]
            res = jnp.dot(rows, right, preferred_element_type=jnp.float32) * scale
            res = res.astype(jnp.bfloat16).reshape(2, BLK, width)
            for s, (_, _, _, dx, dz, other, send) in enumerate(pair):
                tile = res[:, :, s * BLK : (s + 1) * BLK]
                if side == 0:
                    own[k + s] = tile
                    copy = pltpu.make_async_copy(
                        own.at[k + s],
                        out.at[band, :, :, pl.ds(column(dx, dz, other), BLK)],
                        sems.at[k + s],
                    )
                    copy.start()
                    copies.append(copy)
                elif send:
                    sent[at] = tile
                    at += 1
    for copy in copies:
        copy.wait()


def pairs_of(items):
    k = 0
    while k < len(items):
        n = 2 if k + 1 < len(items) and items[k + 1][2] == items[k][2] else 1
        yield k, items[k : k + n]
        k += n


def cross(out, lefts, groups, items, scale, out_shape):
    n, n_sent = len(items), sum(item[6] for item in items)
    first = out is None
    k = lefts[0].shape[2]
    vmem = pl.BlockSpec(memory_space=pltpu.VMEM)
    hbm = pl.BlockSpec(memory_space=pl.ANY)
    return pl.pallas_call(
        functools.partial(cross_body, items, scale, len(groups), first),
        out_shape=[out_shape, jax.ShapeDtypeStruct((n_sent, 2, BLK, BLK), jnp.bfloat16)],
        in_specs=[vmem] * (2 + len(groups)) + ([] if first else [hbm]),
        out_specs=[hbm, vmem],
        scratch_shapes=[
            pltpu.VMEM((n, 2, BLK, BLK), jnp.bfloat16),
            pltpu.SemaphoreType.DMA((n,)),
        ],
        input_output_aliases={} if first else {2 + len(groups): 0},
        cost_estimate=pl.CostEstimate(
            flops=2 * 4 * BLK * k * n * BLK,
            bytes_accessed=n * (k + 4 * BLK) * BLK * 2,
            transcendentals=0,
        ),
        compiler_params=pltpu.CompilerParams(vmem_limit_bytes=20 << 20),
    )(*lefts, *groups, *([] if first else [out]))


def place_body(wheres, *refs):
    n = len(wheres)
    parts, (out, sems) = refs[:n], refs[n + 1 :]
    copies = []
    for part, where in zip(parts, wheres):
        for i, (band, dx, dz) in enumerate(where):
            copy = pltpu.make_async_copy(
                part.at[i],
                out.at[band, :, :, pl.ds(column(dx, dz, True), BLK)],
                sems.at[len(copies)],
            )
            copy.start()
            copies.append(copy)
    for copy in copies:
        copy.wait()


def place(out, parts, wheres):
    count = sum(len(w) for w in wheres)
    hbm = pl.BlockSpec(memory_space=pl.ANY)
    return pl.pallas_call(
        functools.partial(place_body, wheres),
        out_shape=jax.ShapeDtypeStruct(out.shape, out.dtype),
        in_specs=[pl.BlockSpec(memory_space=pltpu.VMEM)] * len(parts) + [hbm],
        out_specs=hbm,
        scratch_shapes=[pltpu.SemaphoreType.DMA((count,))],
        input_output_aliases={len(parts): 0},
        cost_estimate=pl.CostEstimate(
            flops=0, bytes_accessed=count * 4 * BLK * BLK * 2, transcendentals=0
        ),
        compiler_params=pltpu.CompilerParams(vmem_limit_bytes=20 << 20),
    )(*parts, out)


def body(spectra, taps):
    return stack_pairs(features_of(spectra, taps), 1.0 / (spectra.shape[1] * BAND_BINS))


def stack_pairs(features, scale):
    out_shape = jax.ShapeDtypeStruct((2, 2, BLK, 64 * BLK), jnp.bfloat16)

    f0, f1 = features[0], features[1]

    zu1, zd1 = move(f1, dz=1), move(f1, dz=-1)
    x2 = move(features, dx=2)
    partner = move(features, dy=2)
    xm, xp = move(features, dx=1), move(features, dx=-1)
    lefts = (left_rows(features), left_rows(partner))

    zu2, zd2 = move(zu1, dz=1), move(zd1, dz=-1)
    zu3, zd3 = move(zu2, dz=1), move(zd2, dz=-1)
    z4 = move(zu3, dz=1)
    near = jnp.stack([zu1, zd1, zu2, zd2])
    near_dz = (-1, 1, -2, 2)
    nm, np_ = move(near, dx=1), move(near, dx=-1)
    nf = move(nm, dx=1)
    far = jnp.stack([zu3, zd3, z4])
    far_dz = (-3, 3, 4)
    fm, fp = move(far, dx=1), move(far, dx=-1)
    ff = move(fp, dx=-1)

    row = jnp.stack([f0, xm[0], xp[0], x2[0]])
    row_dx = (0, -1, 1, 2)
    up1, dn1 = move(row, dz=1), move(row, dz=-1)
    up2, dn2 = move(up1, dz=1), move(dn1, dz=-1)
    up3, dn3 = move(up2, dz=1), move(dn2, dz=-1)
    up4, dn4 = move(up3[:2], dz=1), move(dn3[2:], dz=-1)

    def at_z(g, dz, dxs=row_dx):
        return [(g, i, 0, dx, dz, False, True) for i, dx in enumerate(dxs)]

    def at_x(g, dx, dzs):
        return [(g, i, 1, dx, dz, False, True) for i, dz in enumerate(dzs)]

    work = [
        (
            [row, xm, xp, x2, near],
            at_z(0, 0)[1:]
            + [(g, 1, 1, dx, 0, False, True) for g, dx in zip((1, 2, 3), row_dx[1:])]
            + at_x(4, 0, near_dz),
        ),
        (
            [nm, np_, far, features, partner],
            at_x(0, -1, near_dz)
            + at_x(1, 1, near_dz)
            + at_x(2, 0, far_dz)
            + [(g, b, b, 0, 0, g == 4, False) for b in (1, 0) for g in (3, 4)],
        ),
        ([fm, fp, up1, dn1], at_x(0, -1, far_dz) + at_x(1, 1, far_dz) + at_z(2, -1) + at_z(3, 1)),
        (
            [nf, ff, up2, dn2],
            at_x(0, 2, near_dz) + at_x(1, 2, far_dz) + at_z(2, -2) + at_z(3, 2),
        ),
        ([up3, dn3], at_z(0, -3) + at_z(1, 3)),
        ([up4, dn4], at_z(0, 4, row_dx[:2]) + at_z(1, 4, row_dx[2:])),
    ]
    out = None
    arrived = []
    for groups, items in work:
        out, sent = cross(out, lefts, groups, items, scale, out_shape)
        got = move(sent, dy=2)
        arrived.append((got, [(i[2], i[3], i[4]) for i in items if i[6]]))
    for part in (arrived[:4], arrived[4:5], arrived[5:]):
        out = place(out, [a[0] for a in part], [a[1] for a in part])
    return out


def solution(mesh):
    split = Mesh(mesh.devices.reshape(SIZES), AXES)
    placed = (P(None, None, BAND, CHAN), P())
    return jax.shard_map(
        body, mesh=split, in_specs=placed, out_specs=P(BAND, None, CHAN, None), check_vma=False
    )
```

```python
import functools

import jax
import jax.numpy as jnp
from jax import lax
from jax.experimental import pallas as pl
from jax.experimental.pallas import tpu as pltpu
from jax.sharding import Mesh, PartitionSpec as P


TAPS = 16
SMOOTH = 5
BAND_BINS = 12
AXES = ("x", "yh", "z", "yl", "core")
SIZES = (4, 2, 8, 2, 2)
CHAN = ("x", "yh", "z")
BAND = ("yl", "core")
BLK = 128
water_level = 0.1


def shifted(dx=0, dy=0, dz=0):
    pairs = []
    for i in range(256):
        core, yl, z, yh, x = i % 2, i // 2 % 2, i // 4 % 8, i // 32 % 2, i // 64
        y = (yh * 2 + yl + dy) % 4
        x, z = (x + dx) % 4, (z + dz) % 8
        pairs.append((i, (((x * 2 + y // 2) * 8 + z) * 2 + y % 2) * 2 + core))
    return pairs


def move(value, **delta):
    return lax.ppermute(value, AXES, shifted(**delta))


def neighbours(axes, wrap):
    devices = lax.axis_size(axes)
    up = [(i, (i + 1) % devices) for i in range(devices if wrap else devices - 1)]
    return up, [(j, i) for i, j in up]


def filter_body(bins_of, x_ref, before_ref, after_ref, taps_ref, *outs):
    start = (lax.axis_index("yl") * 2 + lax.axis_index("core")) * x_ref.shape[1]
    lanes = lax.broadcasted_iota(jnp.int32, x_ref.shape[2:], 1)
    step = 4

    def along(main, halo, lag):
        if lag == 0:
            return main
        inside = lanes >= lag if lag > 0 else lanes < BLK + lag
        return pltpu.roll(jnp.where(inside, main, halo), -lag % BLK, 1)

    def one_bin(first, filt_ref, amp_ref, i, carry):
        f = first + i
        power = None
        for k in range(2):
            x = x_ref[k, f]
            gap = jnp.zeros((x.shape[0], BLK - TAPS), jnp.float32)
            halo = jnp.concatenate([after_ref[k, f], gap, before_ref[k, f]], axis=1)
            mains = [along(x, halo, b) for b in range(step)]
            halos = [along(halo, x, b) for b in range(step)]
            total = None
            for lead in range(0, TAPS, step):
                taps = [taps_ref[(start + f) * TAPS + lead + b] for b in range(step)]
                main = sum(w * v for w, v in zip(taps[1:], mains[1:])) + taps[0] * mains[0]
                side = sum(w * v for w, v in zip(taps[1:], halos[1:])) + taps[0] * halos[0]
                part = along(main, side, lead - TAPS // 2)
                total = part if total is None else total + part
            filt_ref[k, i] = total
            power = total * total if power is None else power + total * total
        amp_ref[i] = jnp.sqrt(power)
        return carry

    for n, (first, count) in enumerate(bins_of):
        filt_ref, amp_ref = outs[2 * n : 2 * n + 2]
        lax.fori_loop(
            0,
            count,
            functools.partial(one_bin, first, filt_ref, amp_ref),
            0,
            unroll=min(count, 4),
        )


def whiten_body(*refs):
    *parts, below_ref, above_ref, feat_ref, ext = refs
    reach = SMOOTH // 2
    ext[:reach] = below_ref[...]
    at = reach
    for n in range(1, len(parts), 2):
        ext[at : at + parts[n].shape[0]] = parts[n][...]
        at += parts[n].shape[0]
    ext[at:] = above_ref[...]
    windows = ext.shape[1]

    def one_bin(first, filt_ref, i, carry):
        f = first + i
        smoothed = jnp.zeros(ext.shape[1:], jnp.float32)
        for d in range(SMOOTH):
            smoothed = smoothed + ext[f + d]
        under = smoothed / SMOOTH + water_level
        band = lax.div(f, BAND_BINS)
        for k in range(2):
            row = pl.multiple_of((k * BAND_BINS + lax.rem(f, BAND_BINS)) * windows, windows)
            feat_ref[band, pl.ds(row, windows)] = (filt_ref[k, i] / under).astype(jnp.bfloat16)
        return carry

    first = 0
    for n in range(0, len(parts), 2):
        count = parts[n].shape[1]
        lax.fori_loop(0, count, functools.partial(one_bin, first, parts[n]), 0, unroll=2)
        first += count


def left_body(feat_ref, left_ref):
    half = feat_ref.shape[1] // 2
    for band in range(2):
        flipped = feat_ref[band].T
        left_ref[band, :BLK] = flipped
        left_ref[band, BLK:] = jnp.concatenate([flipped[:, half:], -flipped[:, :half]], axis=1)


def simple_call(kernel, outs, ins, scratch=(), smem=()):
    vmem = pl.BlockSpec(memory_space=pltpu.VMEM)
    size = sum(v.size * v.dtype.itemsize for v in (*ins, *outs))
    return pl.pallas_call(
        kernel,
        out_shape=outs,
        in_specs=[
            pl.BlockSpec(memory_space=pltpu.SMEM) if i in smem else vmem for i in range(len(ins))
        ],
        out_specs=[vmem] * len(outs),
        scratch_shapes=list(scratch),
        cost_estimate=pl.CostEstimate(flops=4 * size, bytes_accessed=size, transcendentals=0),
        compiler_params=pltpu.CompilerParams(vmem_limit_bytes=20 << 20),
    )(*ins)


def left_rows(features):
    bands, k, c = features.shape
    return simple_call(
        left_body, [jax.ShapeDtypeStruct((bands, 2 * c, k), features.dtype)], [features]
    )[0]


def features_of(spectra, taps):
    edge, reach = TAPS // 2, SMOOTH // 2
    turned = spectra.transpose(0, 2, 1, 3)
    bins, windows, chan = turned.shape[1:]
    up, down = neighbours(CHAN, True)
    last = spectra[..., chan - edge :].transpose(0, 2, 3, 1)
    first = spectra[..., :edge].transpose(0, 2, 3, 1)
    before = lax.ppermute(last, CHAN, up).swapaxes(2, 3)
    after = lax.ppermute(first, CHAN, down).swapaxes(2, 3)
    f32 = jnp.float32
    operands = [turned, before, after, taps.reshape(-1)]

    def filtered(*bins_of):
        shapes = []
        for _, count in bins_of:
            shapes.append(jax.ShapeDtypeStruct((2, count, windows, chan), f32))
            shapes.append(jax.ShapeDtypeStruct((count, windows, chan), f32))
        return simple_call(functools.partial(filter_body, bins_of), shapes, operands, smem=(3,))

    low, low_amp, high, high_amp = filtered((0, reach), (bins - reach, reach))
    up, down = neighbours(BAND, False)
    below = lax.ppermute(high_amp, BAND, up)
    above = lax.ppermute(low_amp, BAND, down)
    mid, mid_amp = filtered((reach, bins - 2 * reach))
    rows = 2 * windows * BAND_BINS
    return simple_call(
        whiten_body,
        [jax.ShapeDtypeStruct((bins // BAND_BINS, rows, chan), jnp.bfloat16)],
        [low, low_amp, mid, mid_amp, high, high_amp, below, above],
        scratch=[pltpu.VMEM((bins + 2 * reach, windows, chan), f32)],
    )[0]


def column(dx, dz, other):
    x = lax.rem(lax.axis_index("x") + (dx % 4), 4)
    yh = lax.axis_index("yh")
    yh = 1 - yh if other else yh
    z = lax.rem(lax.axis_index("z") + (dz % 8), 8)
    return pl.multiple_of(((x * 2 + yh) * 8 + z) * BLK, BLK)


def cross_body(items, scale, n_groups, first, *refs):
    own_left, pair_left = refs[:2]
    groups = refs[2 : 2 + n_groups]
    rest = refs[2 + n_groups :] if first else refs[3 + n_groups :]
    out, sent, own, sems = rest
    copies = []
    at = 0
    for k, pair in pairs_of(items):
        band, both = pair[0][2], any(item[6] for item in pair)
        right = jnp.concatenate(
            [groups[item[0]][... if item[1] == () else item[1]] for item in pair], axis=1
        )
        width = len(pair) * BLK
        for side in range(2 if both else 1):
            rows = (own_left, pair_left)[side][band]
            res = jnp.dot(rows, right, preferred_element_type=jnp.float32) * scale
            res = res.astype(jnp.bfloat16).reshape(2, BLK, width)
            for s, (_, _, _, dx, dz, other, send) in enumerate(pair):
                tile = res[:, :, s * BLK : (s + 1) * BLK]
                if side == 0:
                    own[k + s] = tile
                    copy = pltpu.make_async_copy(
                        own.at[k + s],
                        out.at[band, :, :, pl.ds(column(dx, dz, other), BLK)],
                        sems.at[k + s],
                    )
                    copy.start()
                    copies.append(copy)
                elif send:
                    sent[at] = tile
                    at += 1
    for copy in copies:
        copy.wait()


def pairs_of(items):
    k = 0
    while k < len(items):
        n = 2 if k + 1 < len(items) and items[k + 1][2] == items[k][2] else 1
        yield k, items[k : k + n]
        k += n


def cross(out, lefts, groups, items, scale, out_shape):
    n, n_sent = len(items), sum(item[6] for item in items)
    first = out is None
    k = lefts[0].shape[2]
    vmem = pl.BlockSpec(memory_space=pltpu.VMEM)
    hbm = pl.BlockSpec(memory_space=pl.ANY)
    return pl.pallas_call(
        functools.partial(cross_body, items, scale, len(groups), first),
        out_shape=[out_shape, jax.ShapeDtypeStruct((n_sent, 2, BLK, BLK), jnp.bfloat16)],
        in_specs=[vmem] * (2 + len(groups)) + ([] if first else [hbm]),
        out_specs=[hbm, vmem],
        scratch_shapes=[
            pltpu.VMEM((n, 2, BLK, BLK), jnp.bfloat16),
            pltpu.SemaphoreType.DMA((n,)),
        ],
        input_output_aliases={} if first else {2 + len(groups): 0},
        cost_estimate=pl.CostEstimate(
            flops=2 * 4 * BLK * k * n * BLK,
            bytes_accessed=n * (k + 4 * BLK) * BLK * 2,
            transcendentals=0,
        ),
        compiler_params=pltpu.CompilerParams(vmem_limit_bytes=20 << 20),
    )(*lefts, *groups, *([] if first else [out]))


def place_body(wheres, *refs):
    n = len(wheres)
    parts, (out, sems) = refs[:n], refs[n + 1 :]
    copies = []
    for part, where in zip(parts, wheres):
        for i, (band, dx, dz) in enumerate(where):
            copy = pltpu.make_async_copy(
                part.at[i],
                out.at[band, :, :, pl.ds(column(dx, dz, True), BLK)],
                sems.at[len(copies)],
            )
            copy.start()
            copies.append(copy)
    for copy in copies:
        copy.wait()


def place(out, parts, wheres):
    count = sum(len(w) for w in wheres)
    hbm = pl.BlockSpec(memory_space=pl.ANY)
    return pl.pallas_call(
        functools.partial(place_body, wheres),
        out_shape=jax.ShapeDtypeStruct(out.shape, out.dtype),
        in_specs=[pl.BlockSpec(memory_space=pltpu.VMEM)] * len(parts) + [hbm],
        out_specs=hbm,
        scratch_shapes=[pltpu.SemaphoreType.DMA((count,))],
        input_output_aliases={len(parts): 0},
        cost_estimate=pl.CostEstimate(
            flops=0, bytes_accessed=count * 4 * BLK * BLK * 2, transcendentals=0
        ),
        compiler_params=pltpu.CompilerParams(vmem_limit_bytes=20 << 20),
    )(*parts, out)


def body(spectra, taps):
    return stack_pairs(features_of(spectra, taps), 1.0 / (spectra.shape[1] * BAND_BINS))


def stack_pairs(features, scale):
    out_shape = jax.ShapeDtypeStruct((2, 2, BLK, 64 * BLK), jnp.bfloat16)

    f0, f1 = features[0], features[1]

    zu1, zd1 = move(f1, dz=1), move(f1, dz=-1)
    x2 = move(features, dx=2)
    partner = move(features, dy=2)
    xm, xp = move(features, dx=1), move(features, dx=-1)
    lefts = (left_rows(features), left_rows(partner))

    zu2, zd2 = move(zu1, dz=1), move(zd1, dz=-1)
    zu3, zd3 = move(zu2, dz=1), move(zd2, dz=-1)
    z4 = move(zu3, dz=1)
    near = jnp.stack([zu1, zd1, zu2, zd2])
    near_dz = (-1, 1, -2, 2)
    nm, np_ = move(near, dx=1), move(near, dx=-1)
    nf = move(nm, dx=1)
    far = jnp.stack([zu3, zd3, z4])
    far_dz = (-3, 3, 4)
    fm, fp = move(far, dx=1), move(far, dx=-1)
    ff = move(fp, dx=-1)

    row = jnp.stack([f0, xm[0], xp[0], x2[0]])
    row_dx = (0, -1, 1, 2)
    up1, dn1 = move(row, dz=1), move(row, dz=-1)
    up2, dn2 = move(up1, dz=1), move(dn1, dz=-1)
    up3, dn3 = move(up2, dz=1), move(dn2, dz=-1)
    up4, dn4 = move(up3[:2], dz=1), move(dn3[2:], dz=-1)

    def at_z(g, dz, dxs=row_dx):
        return [(g, i, 0, dx, dz, False, True) for i, dx in enumerate(dxs)]

    def at_x(g, dx, dzs):
        return [(g, i, 1, dx, dz, False, True) for i, dz in enumerate(dzs)]

    work = [
        (
            [xm, xp, x2, zu1, zd1],
            [
                (g, b, b, dx, 0, False, True)
                for b in (0, 1)
                for g, dx in zip((0, 1, 2), row_dx[1:])
            ]
            + [(3, (), 1, 0, -1, False, True), (4, (), 1, 0, 1, False, True)],
        ),
        (
            [zu2, zd2, far],
            [(0, (), 1, 0, -2, False, True), (1, (), 1, 0, 2, False, True)] + at_x(2, 0, far_dz),
        ),
        ([nm, np_], at_x(0, -1, near_dz) + at_x(1, 1, near_dz)),
        ([fm, fp, up1, dn1], at_x(0, -1, far_dz) + at_x(1, 1, far_dz) + at_z(2, -1) + at_z(3, 1)),
        (
            [nf, ff, up2, dn2],
            at_x(0, 2, near_dz) + at_x(1, 2, far_dz) + at_z(2, -2) + at_z(3, 2),
        ),
        (
            [up3, dn3, features, partner],
            at_z(0, -3)
            + at_z(1, 3)
            + [(g, b, b, 0, 0, g == 3, False) for b in (0, 1) for g in (2, 3)],
        ),
        ([up4, dn4], at_z(0, 4, row_dx[:2]) + at_z(1, 4, row_dx[2:])),
    ]
    out = None
    arrived = []
    for groups, items in work:
        out, sent = cross(out, lefts, groups, items, scale, out_shape)
        got = move(sent, dy=2)
        arrived.append((got, [(i[2], i[3], i[4]) for i in items if i[6]]))
    for part in (arrived[:5], arrived[5:6], arrived[6:]):
        out = place(out, [a[0] for a in part], [a[1] for a in part])
    return out


def solution(mesh):
    split = Mesh(mesh.devices.reshape(SIZES), AXES)
    placed = (P(None, None, BAND, CHAN), P())
    return jax.shard_map(
        body, mesh=split, in_specs=placed, out_specs=P(BAND, None, CHAN, None), check_vma=False
    )
```

```python
import functools

import jax
import jax.numpy as jnp
from jax import lax
from jax.experimental import pallas as pl
from jax.experimental.pallas import tpu as pltpu
from jax.sharding import Mesh, PartitionSpec as P


TAPS = 16
SMOOTH = 5
BAND_BINS = 12
AXES = ("x", "yh", "z", "yl", "core")
SIZES = (4, 2, 8, 2, 2)
CHAN = ("x", "yh", "z")
BAND = ("yl", "core")
BLK = 128
water_level = 0.1


def shifted(dx=0, dy=0, dz=0):
    pairs = []
    for i in range(256):
        core, yl, z, yh, x = i % 2, i // 2 % 2, i // 4 % 8, i // 32 % 2, i // 64
        y = (yh * 2 + yl + dy) % 4
        x, z = (x + dx) % 4, (z + dz) % 8
        pairs.append((i, (((x * 2 + y // 2) * 8 + z) * 2 + y % 2) * 2 + core))
    return pairs


def move(value, **delta):
    return lax.ppermute(value, AXES, shifted(**delta))


def neighbours(axes, wrap):
    devices = lax.axis_size(axes)
    up = [(i, (i + 1) % devices) for i in range(devices if wrap else devices - 1)]
    return up, [(j, i) for i, j in up]


LANE_GROUPS = BLK // (TAPS // 2)


def pack_body(x_ref, first_ref, last_ref):
    edge = TAPS // 2
    rows = x_ref.shape[0] * x_ref.shape[2]
    place = lax.broadcasted_iota(jnp.int32, (rows, BLK), 1) // edge
    for g in range(first_ref.shape[1]):
        ends = [jnp.zeros((rows, BLK), jnp.float32) for _ in range(2)]
        for j in range(min(LANE_GROUPS, x_ref.shape[1] - g * LANE_GROUPS)):
            x = x_ref[:, g * LANE_GROUPS + j].reshape(rows, BLK)
            for n, lead in enumerate((0, BLK - edge)):
                shift = (j * edge - lead) % BLK
                ends[n] = jnp.where(place == j, pltpu.roll(x, shift, 1) if shift else x, ends[n])
        first_ref[:, g] = ends[0].reshape(x_ref.shape[0], x_ref.shape[2], BLK)
        last_ref[:, g] = ends[1].reshape(x_ref.shape[0], x_ref.shape[2], BLK)


def filter_body(bins_of, x_ref, before_ref, after_ref, taps_ref, *outs):
    start = (lax.axis_index("yl") * 2 + lax.axis_index("core")) * x_ref.shape[1]
    parts, windows = x_ref.shape[0], x_ref.shape[2]
    rows = parts * windows
    lanes = lax.broadcasted_iota(jnp.int32, (rows, BLK), 1)
    step, edge = 4, TAPS // 2

    def along(main, halo, lag):
        if lag == 0:
            return main
        inside = lanes >= lag if lag > 0 else lanes < BLK + lag
        return pltpu.roll(jnp.where(inside, main, halo), -lag % BLK, 1)

    def one_bin(first, filt_ref, amp_ref, i, carry):
        f = first + i
        x = x_ref[:, f].reshape(rows, BLK)
        g, lead = lax.div(f, LANE_GROUPS), lax.rem(f, LANE_GROUPS) * edge
        after = pltpu.roll(after_ref[:, g].reshape(rows, BLK), lax.rem(BLK - lead, BLK), 1)
        before = pltpu.roll(before_ref[:, g].reshape(rows, BLK), BLK - edge - lead, 1)
        halo = jnp.where(lanes < edge, after, before)
        mains = [along(x, halo, b) for b in range(step)]
        halos = [along(halo, x, b) for b in range(step)]
        total = None
        for lead in range(0, TAPS, step):
            taps = [taps_ref[(start + f) * TAPS + lead + b] for b in range(step)]
            main, side = taps[0] * mains[0], taps[0] * halos[0]
            for b in range(1, step):
                main, side = main + taps[b] * mains[b], side + taps[b] * halos[b]
            part = along(main, side, lead - edge)
            total = part if total is None else total + part
        total = total.reshape(parts, windows, BLK)
        filt_ref[:, i] = total
        amp_ref[i] = jnp.sqrt(total[0] * total[0] + total[1] * total[1])
        return carry

    for n, (first, count) in enumerate(bins_of):
        filt_ref, amp_ref = outs[2 * n : 2 * n + 2]
        lax.fori_loop(
            0,
            count,
            functools.partial(one_bin, first, filt_ref, amp_ref),
            0,
            unroll=min(count, 4),
        )


def whiten_body(*refs):
    *parts, below_ref, above_ref, feat_ref, ext = refs
    reach = SMOOTH // 2
    ext[:reach] = below_ref[...]
    at = reach
    for n in range(1, len(parts), 2):
        ext[at : at + parts[n].shape[0]] = parts[n][...]
        at += parts[n].shape[0]
    ext[at:] = above_ref[...]
    windows = ext.shape[1]

    def one_bin(first, filt_ref, i, carry):
        f = first + i
        smoothed = jnp.zeros(ext.shape[1:], jnp.float32)
        for d in range(SMOOTH):
            smoothed = smoothed + ext[f + d]
        under = smoothed / SMOOTH + water_level
        band = lax.div(f, BAND_BINS)
        for k in range(2):
            row = pl.multiple_of((k * BAND_BINS + lax.rem(f, BAND_BINS)) * windows, windows)
            feat_ref[band, pl.ds(row, windows)] = (filt_ref[k, i] / under).astype(jnp.bfloat16)
        return carry

    first = 0
    for n in range(0, len(parts), 2):
        count = parts[n].shape[1]
        lax.fori_loop(0, count, functools.partial(one_bin, first, parts[n]), 0, unroll=2)
        first += count


def left_body(feat_ref, left_ref):
    half = feat_ref.shape[1] // 2
    for band in range(2):
        flipped = feat_ref[band].T
        left_ref[band, :BLK] = flipped
        left_ref[band, BLK:] = jnp.concatenate([flipped[:, half:], -flipped[:, :half]], axis=1)


def simple_call(kernel, outs, ins, scratch=(), smem=()):
    vmem = pl.BlockSpec(memory_space=pltpu.VMEM)
    size = sum(v.size * v.dtype.itemsize for v in (*ins, *outs))
    return pl.pallas_call(
        kernel,
        out_shape=outs,
        in_specs=[
            pl.BlockSpec(memory_space=pltpu.SMEM) if i in smem else vmem for i in range(len(ins))
        ],
        out_specs=[vmem] * len(outs),
        scratch_shapes=list(scratch),
        cost_estimate=pl.CostEstimate(flops=4 * size, bytes_accessed=size, transcendentals=0),
        compiler_params=pltpu.CompilerParams(vmem_limit_bytes=20 << 20),
    )(*ins)


def left_rows(features):
    bands, k, c = features.shape
    return simple_call(
        left_body, [jax.ShapeDtypeStruct((bands, 2 * c, k), features.dtype)], [features]
    )[0]


def features_of(spectra, taps):
    reach = SMOOTH // 2
    turned = spectra.transpose(0, 2, 1, 3)
    parts, bins, windows, chan = turned.shape
    ends = jax.ShapeDtypeStruct((parts, pl.cdiv(bins, LANE_GROUPS), windows, chan), jnp.float32)
    first, last = simple_call(pack_body, [ends, ends], [turned])
    up, down = neighbours(CHAN, True)
    before = lax.ppermute(last, CHAN, up)
    after = lax.ppermute(first, CHAN, down)
    f32 = jnp.float32
    operands = [turned, before, after, taps.reshape(-1)]

    def filtered(*bins_of):
        shapes = []
        for _, count in bins_of:
            shapes.append(jax.ShapeDtypeStruct((2, count, windows, chan), f32))
            shapes.append(jax.ShapeDtypeStruct((count, windows, chan), f32))
        return simple_call(functools.partial(filter_body, bins_of), shapes, operands, smem=(3,))

    low, low_amp, high, high_amp = filtered((0, reach), (bins - reach, reach))
    up, down = neighbours(BAND, False)
    below = lax.ppermute(high_amp, BAND, up)
    above = lax.ppermute(low_amp, BAND, down)
    mid, mid_amp = filtered((reach, bins - 2 * reach))
    rows = 2 * windows * BAND_BINS
    return simple_call(
        whiten_body,
        [jax.ShapeDtypeStruct((bins // BAND_BINS, rows, chan), jnp.bfloat16)],
        [low, low_amp, mid, mid_amp, high, high_amp, below, above],
        scratch=[pltpu.VMEM((bins + 2 * reach, windows, chan), f32)],
    )[0]


def column(dx, dz, other):
    x = lax.rem(lax.axis_index("x") + (dx % 4), 4)
    yh = lax.axis_index("yh")
    yh = 1 - yh if other else yh
    z = lax.rem(lax.axis_index("z") + (dz % 8), 8)
    return pl.multiple_of(((x * 2 + yh) * 8 + z) * BLK, BLK)


def cross_body(items, scale, n_groups, first, *refs):
    own_left, pair_left = refs[:2]
    groups = refs[2 : 2 + n_groups]
    rest = refs[2 + n_groups :] if first else refs[3 + n_groups :]
    out, sent, own, sems = rest
    copies = []
    at = 0
    for k, pair in pairs_of(items):
        band, both = pair[0][2], any(item[6] for item in pair)
        right = jnp.concatenate(
            [groups[item[0]][... if item[1] == () else item[1]] for item in pair], axis=1
        )
        width = len(pair) * BLK
        for side in range(2 if both else 1):
            rows = (own_left, pair_left)[side][band]
            res = jnp.dot(rows, right, preferred_element_type=jnp.float32) * scale
            res = res.astype(jnp.bfloat16).reshape(2, BLK, width)
            for s, (_, _, _, dx, dz, other, send) in enumerate(pair):
                tile = res[:, :, s * BLK : (s + 1) * BLK]
                if side == 0:
                    own[k + s] = tile
                    copy = pltpu.make_async_copy(
                        own.at[k + s],
                        out.at[band, :, :, pl.ds(column(dx, dz, other), BLK)],
                        sems.at[k + s],
                    )
                    copy.start()
                    copies.append(copy)
                elif send:
                    sent[at] = tile
                    at += 1
    for copy in copies:
        copy.wait()


def pairs_of(items):
    k = 0
    while k < len(items):
        n = 2 if k + 1 < len(items) and items[k + 1][2] == items[k][2] else 1
        yield k, items[k : k + n]
        k += n


def cross(out, lefts, groups, items, scale, out_shape):
    n, n_sent = len(items), sum(item[6] for item in items)
    first = out is None
    k = lefts[0].shape[2]
    vmem = pl.BlockSpec(memory_space=pltpu.VMEM)
    hbm = pl.BlockSpec(memory_space=pl.ANY)
    return pl.pallas_call(
        functools.partial(cross_body, items, scale, len(groups), first),
        out_shape=[out_shape, jax.ShapeDtypeStruct((n_sent, 2, BLK, BLK), jnp.bfloat16)],
        in_specs=[vmem] * (2 + len(groups)) + ([] if first else [hbm]),
        out_specs=[hbm, vmem],
        scratch_shapes=[
            pltpu.VMEM((n, 2, BLK, BLK), jnp.bfloat16),
            pltpu.SemaphoreType.DMA((n,)),
        ],
        input_output_aliases={} if first else {2 + len(groups): 0},
        cost_estimate=pl.CostEstimate(
            flops=2 * 4 * BLK * k * n * BLK,
            bytes_accessed=n * (k + 4 * BLK) * BLK * 2,
            transcendentals=0,
        ),
        compiler_params=pltpu.CompilerParams(vmem_limit_bytes=20 << 20),
    )(*lefts, *groups, *([] if first else [out]))


def place_body(wheres, *refs):
    n = len(wheres)
    parts, (out, sems) = refs[:n], refs[n + 1 :]
    copies = []
    for part, where in zip(parts, wheres):
        for i, (band, dx, dz) in enumerate(where):
            copy = pltpu.make_async_copy(
                part.at[i],
                out.at[band, :, :, pl.ds(column(dx, dz, True), BLK)],
                sems.at[len(copies)],
            )
            copy.start()
            copies.append(copy)
    for copy in copies:
        copy.wait()


def place(out, parts, wheres):
    count = sum(len(w) for w in wheres)
    hbm = pl.BlockSpec(memory_space=pl.ANY)
    return pl.pallas_call(
        functools.partial(place_body, wheres),
        out_shape=jax.ShapeDtypeStruct(out.shape, out.dtype),
        in_specs=[pl.BlockSpec(memory_space=pltpu.VMEM)] * len(parts) + [hbm],
        out_specs=hbm,
        scratch_shapes=[pltpu.SemaphoreType.DMA((count,))],
        input_output_aliases={len(parts): 0},
        cost_estimate=pl.CostEstimate(
            flops=0, bytes_accessed=count * 4 * BLK * BLK * 2, transcendentals=0
        ),
        compiler_params=pltpu.CompilerParams(vmem_limit_bytes=20 << 20),
    )(*parts, out)


def body(spectra, taps):
    return stack_pairs(features_of(spectra, taps), 1.0 / (spectra.shape[1] * BAND_BINS))


def stack_pairs(features, scale):
    out_shape = jax.ShapeDtypeStruct((2, 2, BLK, 64 * BLK), jnp.bfloat16)

    f0, f1 = features[0], features[1]

    zu1, zd1 = move(f1, dz=1), move(f1, dz=-1)
    x2 = move(features, dx=2)
    partner = move(features, dy=2)
    xm, xp = move(features, dx=1), move(features, dx=-1)
    lefts = (left_rows(features), left_rows(partner))

    zu2, zd2 = move(zu1, dz=1), move(zd1, dz=-1)
    zu3, zd3 = move(zu2, dz=1), move(zd2, dz=-1)
    z4 = move(zu3, dz=1)
    near = jnp.stack([zu1, zd1, zu2, zd2])
    near_dz = (-1, 1, -2, 2)
    nm, np_ = move(near, dx=1), move(near, dx=-1)
    nf = move(nm, dx=1)
    far = jnp.stack([zu3, zd3, z4])
    far_dz = (-3, 3, 4)
    fm, fp = move(far, dx=1), move(far, dx=-1)
    ff = move(fp, dx=-1)

    row = jnp.stack([f0, xm[0], xp[0], x2[0]])
    row_dx = (0, -1, 1, 2)
    up1, dn1 = move(row, dz=1), move(row, dz=-1)
    up2, dn2 = move(up1, dz=1), move(dn1, dz=-1)
    up3, dn3 = move(up2, dz=1), move(dn2, dz=-1)
    up4, dn4 = move(up3[:2], dz=1), move(dn3[2:], dz=-1)

    def at_z(g, dz, dxs=row_dx):
        return [(g, i, 0, dx, dz, False, True) for i, dx in enumerate(dxs)]

    def at_x(g, dx, dzs):
        return [(g, i, 1, dx, dz, False, True) for i, dz in enumerate(dzs)]

    work = [
        (
            [xm, xp, x2, zu1, zd1],
            [
                (g, b, b, dx, 0, False, True)
                for b in (0, 1)
                for g, dx in zip((0, 1, 2), row_dx[1:])
            ]
            + [(3, (), 1, 0, -1, False, True), (4, (), 1, 0, 1, False, True)],
        ),
        (
            [zu2, zd2, far],
            [(0, (), 1, 0, -2, False, True), (1, (), 1, 0, 2, False, True)] + at_x(2, 0, far_dz),
        ),
        ([nm, np_], at_x(0, -1, near_dz) + at_x(1, 1, near_dz)),
        ([fm, fp, up1, dn1], at_x(0, -1, far_dz) + at_x(1, 1, far_dz) + at_z(2, -1) + at_z(3, 1)),
        (
            [nf, ff, up2, dn2],
            at_x(0, 2, near_dz) + at_x(1, 2, far_dz) + at_z(2, -2) + at_z(3, 2),
        ),
        (
            [up3, dn3, features, partner],
            at_z(0, -3)
            + at_z(1, 3)
            + [(g, b, b, 0, 0, g == 3, False) for b in (0, 1) for g in (2, 3)],
        ),
        ([up4, dn4], at_z(0, 4, row_dx[:2]) + at_z(1, 4, row_dx[2:])),
    ]
    out = None
    arrived = []
    for groups, items in work:
        out, sent = cross(out, lefts, groups, items, scale, out_shape)
        got = move(sent, dy=2)
        arrived.append((got, [(i[2], i[3], i[4]) for i in items if i[6]]))
    for part in (arrived[:5], arrived[5:6], arrived[6:]):
        out = place(out, [a[0] for a in part], [a[1] for a in part])
    return out


def solution(mesh):
    split = Mesh(mesh.devices.reshape(SIZES), AXES)
    placed = (P(None, None, BAND, CHAN), P())
    return jax.shard_map(
        body, mesh=split, in_specs=placed, out_specs=P(BAND, None, CHAN, None), check_vma=False
    )
```
